32 devices in a mesh: chain: 8 (over z, y), col: 4 (over x, core).
Axes of the slice: x: 2, y: 2, z: 4, core: 2. Of those that a mesh axis runs over, the one named last changes fastest.
Arguments:
- rhs: bfloat16 [4, 8, 32, 128], P(None, 'chain'), may hold values from -6 to 6
- pattern: int32 [4, 8, 24], P(None, 'chain', 'col'), may hold values from 0 to 31, as said below
- factor: bfloat16 [4, 8, 24, 128, 128], P(None, 'chain', 'col'), may hold values from -0.1875 to 0.1875
- inverse: bfloat16 [4, 8, 128, 128], P(None, 'chain'), as said below
- level_size: int32 [6], replicated, may hold values from 1 to 8, 32 in all
Outputs:
- half_solved: bfloat16 [4, 8, 32, 128], P(None, 'chain')
- solved: bfloat16 [4, 8, 32, 128], P(None, 'chain')
The draws below stay inside these ranges and needn't reach their ends.
Inputs may be any that keep to these rules, and one draw needn't show every extreme that they name: Among the pattern entries held by one index of chain and one index of col (all 4 of its block rows), at most 3 name block rows on any one index of chain (block row mod 8); in every such group exactly 3 name block rows on one index of chain that is common to all groups of that index of col. A block row may name a block row more than once. `inverse`: each block is lower triangular with a diagonal between 0.3 and 2.
All inputs are finite; a program needn't handle non-finite values.
Results may differ from the reference program's by a relative error of at most 0.013.
Values may be sent and summed in bfloat16 or wider, within the bound.
A program may use at most 64 MiB of HBM per device.

```python
import math
import jax
import jax.numpy as jnp
import numpy as np
from jax import lax

BLOCK = 128
NNZ = 24
PROBES = 32
ROWS_DEV = 4
LEVELS = 6
BLOCK_ROWS = 32
CAP = 3
N_CHAIN = 8
N_COL = 4


def draw_pattern(key, part):
    entries = NNZ // N_COL
    count = ROWS_DEV * entries
    runs = (count + CAP - 1) // CAP
    key_first = jax.random.fold_in(key, 21)
    key_perm = jax.random.fold_in(key, 22)
    key_base = jax.random.fold_in(key, 23)
    first = jax.random.randint(key_first, (N_COL,), 0, N_CHAIN, dtype=jnp.int32)
    group_keys = jax.random.split(key_perm, N_CHAIN * N_COL)
    others = jax.vmap(lambda single: jax.random.permutation(single, N_CHAIN - 1))(group_keys)
    others = others.astype(jnp.int32).reshape(N_CHAIN, N_COL, N_CHAIN - 1)
    firsts = jnp.broadcast_to(first[None, :, None], (N_CHAIN, N_COL, 1))
    order = jnp.concatenate([firsts, (firsts + 1 + others) % N_CHAIN], axis=2)
    positions = jnp.arange(count, dtype=jnp.int32)
    run_ids = positions // CAP
    lane = order[:, :, run_ids]
    base = jax.random.randint(key_base, (N_CHAIN, N_COL, runs), 0, ROWS_DEV, dtype=jnp.int32)
    quotient = (base[:, :, run_ids] + (positions % CAP)[None, None, :]) % ROWS_DEV
    column = quotient * N_CHAIN + lane
    column = column.reshape(N_CHAIN, N_COL, ROWS_DEV, entries).transpose(2, 0, 1, 3)
    return column.reshape(ROWS_DEV, N_CHAIN, NNZ).astype(jnp.int32)


def draw_inverse(key, part):
    key_diag = jax.random.fold_in(key, 11)
    key_low = jax.random.fold_in(key, 12)
    diagonal = jax.random.uniform(key_diag, (ROWS_DEV, N_CHAIN, BLOCK), jnp.float32, 0.5, 1.5)
    lower = jax.random.normal(key_low, (ROWS_DEV, N_CHAIN, BLOCK, BLOCK), jnp.float32)
    lower = jnp.tril(lower, -1) * (0.6 / jnp.sqrt(BLOCK * 1.0))
    eye = jnp.eye(BLOCK, dtype=jnp.float32)
    return (lower + diagonal[..., None] * eye).astype(jnp.bfloat16)


def level_of(key, extent, shards, smallest, largest):
    def one(axis_at, blocks):
        steps = jax.random.uniform(jax.random.fold_in(jax.random.fold_in(key, 6), axis_at), (blocks,), jnp.float32, smallest / len(shards), largest / len(shards))
        return jnp.repeat(jnp.exp(steps), extent[axis_at] // blocks).reshape((-1,) + (1,) * (len(extent) - axis_at - 1))

    level = one(*shards[0])
    for cut in shards[1:]:
        level = level * one(*cut)
    return level


def split_up(number_of, total, bound, lean):
    weights = [(1 << 20) // math.isqrt(grade ** lean) + 1 for grade in range(2, number_of + 1)]
    spare, counts = total - bound - (number_of - 1), [1] * (number_of - 1)
    while spare > 0:
        movable = [i for i in range(number_of - 1) if counts[i] < bound]
        whole, remaining = sum([weights[i] for i in movable]), spare
        for i in movable:
            extra = min(bound - counts[i], max(1, remaining * weights[i] // whole), spare)
            counts[i] = counts[i] + extra
            spare = spare - extra
    return np.array([bound] + counts)


def uneven(own_key, amount, total, most, slope):
    if amount == 2:
        one = jax.random.randint(own_key, (), max(1, total - most), min(most, total - 1) + 1)
        return jnp.stack([one, total - one])
    sizes = jnp.asarray(split_up(amount, total, most, slope), jnp.int32)
    couples = (amount - 1) // 2
    donor, taker = sizes[1:1 + 2 * couples:2], sizes[2:2 + 2 * couples:2]
    margin = jnp.minimum(donor - 1, most - taker)
    passed = jax.random.randint(jax.random.fold_in(own_key, 1), (couples,), 0, 1 << 20) % (margin + 1)
    sizes = sizes.at[1:1 + 2 * couples:2].set(donor - passed).at[2:2 + 2 * couples:2].set(taker + passed)
    return sizes[jax.random.permutation(jax.random.fold_in(own_key, 2), amount)]


def scatter_about(stream_key, shape, width, limit, cuts=(), held_as=jnp.bfloat16):
    result = width * jax.random.normal(stream_key, shape, jnp.float32)
    if cuts:
        result = result * level_of(stream_key, shape, cuts, -0.22, 0.18)
    return jnp.clip(result, -limit, limit).astype(held_as)


def setup_inputs(seed: int = 0) -> dict:
    seeds = jax.random.split(jax.random.key(seed), 6)
    rhs = scatter_about(seeds[0], (ROWS_DEV, N_CHAIN, PROBES, BLOCK), 1.0, 6.0, ((1, 8),))
    pattern = draw_pattern(jax.random.fold_in(seeds[5], 71), 0)
    factor = scatter_about(seeds[2], (ROWS_DEV, N_CHAIN, NNZ, BLOCK, BLOCK), (BLOCK * NNZ // 3) ** -0.5, 0.1875, ((1, 8), (2, 4)))
    inverse = draw_inverse(jax.random.fold_in(seeds[5], 71), 0)
    level_size = uneven(seeds[4], LEVELS, BLOCK_ROWS, N_CHAIN, 0).astype(jnp.int32)
    return {"rhs": rhs, "pattern": pattern, "factor": factor, "inverse": inverse, "level_size": level_size}


def level_index(positions, ends):
    return jnp.sum((positions[..., None] >= ends).astype(jnp.int32), axis=-1)


def reference(rhs, pattern, factor, inverse, level_size):
    total = ROWS_DEV * N_CHAIN
    right = rhs.reshape(total, PROBES, BLOCK)
    columns = pattern.reshape(total, NNZ).astype(jnp.int32)
    blocks = factor.reshape(total, NNZ, BLOCK, BLOCK)
    inverse_rows = inverse.reshape(total, BLOCK, BLOCK)
    ends = jnp.cumsum(level_size).astype(jnp.int32)
    row_level = level_index(jnp.arange(total, dtype=jnp.int32), ends)
    keep = level_index(columns, ends) < row_level[:, None]

    def forward(store, row_id):
        chosen = jnp.where(keep[row_id][:, None, None], store[columns[row_id]], 0).astype(jnp.float32)
        partial_value = jnp.einsum("jpb,jcb->pc", chosen, blocks[row_id].astype(jnp.float32), precision=lax.Precision.HIGHEST)
        rest = (right[row_id].astype(jnp.float32) - partial_value).astype(jnp.bfloat16)
        segment = jnp.dot(rest, inverse_rows[row_id].T, preferred_element_type=jnp.float32).astype(jnp.bfloat16)
        return store.at[row_id].set(segment), None

    store, _ = lax.scan(forward, jnp.zeros((total, PROBES, BLOCK), jnp.bfloat16), jnp.arange(total, dtype=jnp.int32))

    def backward(accum, row_id):
        rest = (store[row_id].astype(jnp.float32) - accum[row_id]).astype(jnp.bfloat16)
        segment = jnp.dot(rest, inverse_rows[row_id], preferred_element_type=jnp.float32).astype(jnp.bfloat16)
        terms = jnp.einsum("pc,jcb->jpb", segment.astype(jnp.float32), blocks[row_id].astype(jnp.float32), precision=lax.Precision.HIGHEST)
        terms = jnp.where(keep[row_id][:, None, None], terms, 0.0)
        accum = accum.at[columns[row_id]].add(terms)
        return accum, segment

    _, solved = lax.scan(backward, jnp.zeros((total, PROBES, BLOCK), jnp.float32), jnp.arange(total, dtype=jnp.int32), reverse=True)
    return store.reshape(rhs.shape), solved.reshape(rhs.shape)
```

```python
import functools

import jax
import jax.numpy as jnp
from jax import lax
from jax.experimental import pallas as pl
from jax.experimental.pallas import tpu as pltpu
from jax.sharding import PartitionSpec as P

MESH = pl.DeviceIdType.MESH
F32 = jnp.float32
BF16 = jnp.bfloat16


def kernel(
    n_chain,
    n_col,
    levels,
    rhs_ref,
    pat_ref,
    fac_ref,
    inv_ref,
    size_ref,
    half_out,
    solved_out,
    fb,
    pat_v,
    pat_s,
    code_s,
    rhs_f,
    store,
    seg_send,
    seg_recv,
    acc,
    acc_recv,
    half_lv,
    sol_lv,
    half_tx,
    sol_tx,
    half_rx,
    sol_rx,
    pat_sem,
    pat_ssem,
    pat_lsem,
    loc_sem,
    fx_send,
    fx_recv,
    fo_send,
    fo_recv,
    ff_send,
    ff_recv,
    sg_send,
    sg_recv,
    ac_send,
    ac_recv,
    ho_send,
    ho_recv,
    so_send,
    so_recv,
):
    rows = rhs_ref.shape[0]
    probes = rhs_ref.shape[2]
    width = rhs_ref.shape[3]
    part = probes // n_col
    entries = fac_ref.shape[2]
    total = entries * n_col
    me = lax.axis_index("chain")
    k = lax.axis_index("col")
    far = lax.rem(k + n_col // 2, n_col)
    near = k + 1 - 2 * lax.rem(k, 2)
    near_far = lax.rem(near + n_col // 2, n_col)

    def lane(d):
        return lax.rem(me + d, n_chain)

    def column(d):
        return lax.rem(k + d, n_col)

    barrier = pltpu.get_barrier_semaphore()
    for d in range(1, n_chain):
        pl.semaphore_signal(barrier, inc=1, device_id={"chain": lane(d)}, device_id_type=MESH)
    for d in range(1, n_col):
        pl.semaphore_signal(barrier, inc=1, device_id={"col": column(d)}, device_id_type=MESH)
    pl.semaphore_wait(barrier, n_chain + n_col - 2)

    pat_copies = []
    for d in range(1, n_col):
        pat_copies.append(
            pltpu.make_async_remote_copy(
                src_ref=pat_ref,
                dst_ref=pat_v.at[d],
                send_sem=pat_ssem.at[d],
                recv_sem=pat_sem.at[d],
                device_id={"col": column(d)},
                device_id_type=MESH,
            )
        )
    for copy in pat_copies:
        copy.start()
    pat_local = [pltpu.make_async_copy(pat_ref, pat_s.at[0], pat_lsem.at[0])]
    pat_local[0].start()

    def held(row, who):
        return fb.at[row, pl.ds(who * entries, entries)]

    far_copies = []
    near_copies = []
    forwards = []
    locals_ = []
    for row in range(rows):
        far_copies.append(
            pltpu.make_async_remote_copy(
                src_ref=fac_ref.at[row, 0],
                dst_ref=held(row, k),
                send_sem=fx_send.at[row],
                recv_sem=fx_recv.at[row],
                device_id={"col": far},
                device_id_type=MESH,
            )
        )
        near_copies.append(
            pltpu.make_async_remote_copy(
                src_ref=fac_ref.at[row, 0],
                dst_ref=held(row, k),
                send_sem=fo_send.at[row],
                recv_sem=fo_recv.at[row],
                device_id={"col": near},
                device_id_type=MESH,
            )
        )
        forwards.append(
            pltpu.make_async_remote_copy(
                src_ref=held(row, far),
                dst_ref=held(row, far),
                send_sem=ff_send.at[row],
                recv_sem=ff_recv.at[row],
                device_id={"col": near},
                device_id_type=MESH,
            )
        )
        locals_.append(
            pltpu.make_async_copy(fac_ref.at[row, 0], held(row, k), loc_sem.at[row])
        )
    for copy in far_copies:
        copy.start()

    ends = []
    running = jnp.int32(0)
    for level in range(levels):
        running = running + size_ref[level]
        ends.append(running)

    def level_of(position):
        found = jnp.int32(0)
        for end in ends[:-1]:
            found = found + (position >= end).astype(jnp.int32)
        return found

    own_level = [level_of(row * n_chain + me) for row in range(rows)]
    slot = []
    live = []
    for level in range(levels):
        here = jnp.int32(0)
        count = jnp.int32(0)
        for row in range(rows):
            match = own_level[row] == level
            here = jnp.where(match, row, here)
            count = count + match.astype(jnp.int32)
        slot.append(here)
        live.append(count > 0)

    for row in range(rows):
        rhs_f[row] = rhs_ref[row, 0].astype(F32)

    def finish_forward(level, sums):
        right = rhs_f[slot[level], pl.ds(k * part, part), :]
        rest = (right - sums if sums is not None else right).astype(BF16)
        segment = lax.dot_general(
            rest, inv_ref[slot[level], 0], (((1,), (1,)), ((), ())), preferred_element_type=F32
        ).astype(BF16)
        copies = []
        if level < levels - 1:
            seg_send[level] = segment
            for d in range(1, n_chain):
                copies.append(
                    pltpu.make_async_remote_copy(
                        src_ref=seg_send.at[level],
                        dst_ref=seg_recv.at[level, d],
                        send_sem=sg_send.at[level, d],
                        recv_sem=sg_recv.at[level, d],
                        device_id={"chain": lane(d)},
                        device_id_type=MESH,
                    )
                )
            for copy in copies:
                copy.start()
        wide = segment.astype(F32)
        half_lv[level] = wide
        if level < levels - 1:
            store[level * n_chain + me] = wide
        return copies

    pending = []
    copies = finish_forward(0, None)
    for copy in near_copies:
        copy.start()
    for copy in locals_:
        copy.start()
    own = copies
    store[pl.ds(n_chain, (levels - 1) * n_chain)] = jnp.zeros(
        ((levels - 1) * n_chain, part, width), F32
    )
    acc[...] = jnp.zeros_like(acc)

    for d in range(1, n_col):
        pat_copies[d - 1].wait_recv()
        copy = pltpu.make_async_copy(pat_v.at[d], pat_s.at[d], pat_lsem.at[d])
        copy.start()
        pat_local.append(copy)
    for copy in pat_local:
        copy.wait()

    for level in range(1, levels):
        def fill(place, carry, level=level):
            who = lax.div(place, entries)
            item = lax.rem(place, entries)
            d = lax.rem(k - who + n_col, n_col)
            target = pat_s[d, slot[level], 0, item]
            code_s[level, place] = level_of(target) * n_chain + lax.rem(target, n_chain)
            return carry
        for place in range(total):
            fill(jnp.int32(place), 0)

    ready = [False] * rows

    def make_ready(upto):
        todo = [row for row in range(upto + 1) if not ready[row]]
        for row in todo:
            far_copies[row].wait_recv()
            forwards[row].start()
        for row in todo:
            locals_[row].wait()
            near_copies[row].wait_recv()
            forwards[row].wait_recv()
            ready[row] = True

    def times_rows(pieces, row):
        sums = None
        for j in range(0, total, 2):
            left = jnp.concatenate([pieces[j], pieces[j + 1]], axis=1)
            right = jnp.concatenate([fb[row, j], fb[row, j + 1]], axis=1)
            term = lax.dot_general(
                left, right, (((1,), (1,)), ((), ())), preferred_element_type=F32
            )
            sums = term if sums is None else sums + term
        return sums

    for level in range(1, levels):
        make_ready(min(level, rows - 1))
        for d in range(1, n_chain):
            own[d - 1].wait_recv()
            store[(level - 1) * n_chain + lane(n_chain - d)] = seg_recv[level - 1, d].astype(F32)
        pending += own
        pieces = [store[code_s[level, j]].astype(BF16) for j in range(total)]
        if level >= rows - 1:
            sums = times_rows(pieces, slot[level])
        else:
            sums = jnp.zeros((part, width), F32)
            for row in range(level + 1):
                sums = sums + jnp.where(slot[level] == row, times_rows(pieces, row), 0.0)
        own = finish_forward(level, sums)

    def share(tx, rx, by_level, send, recv):
        for row in range(rows):
            tx[row] = by_level[own_level[row]].astype(BF16)
        copies = [
            pltpu.make_async_remote_copy(
                src_ref=tx,
                dst_ref=rx.at[d],
                send_sem=send.at[d],
                recv_sem=recv.at[d],
                device_id={"col": column(d)},
                device_id_type=MESH,
            )
            for d in range(1, n_col)
        ]
        for copy in copies:
            copy.start()
        return copies

    group = lax.broadcasted_iota(jnp.int32, (n_chain * part, width), 0) // part
    half_copies = []
    own = []
    for level in reversed(range(levels)):
        rest = half_lv[level]
        if level < levels - 1:
            rest = rest - acc[level, pl.ds(me * part, part)]
            for d in range(1, n_chain):
                own[d - 1].wait_recv()
                rest = rest - acc_recv[level, d]
            pending += own
        solved = jnp.dot(
            rest.astype(BF16), inv_ref[slot[level], 0], preferred_element_type=F32
        ).astype(BF16).astype(F32)
        sol_lv[level] = solved
        if level == 0:
            break
        solved = jnp.where(live[level], solved, 0.0)
        tiled = jnp.concatenate([solved] * n_chain, axis=0)

        def spread(target, tiled=tiled, level=level):
            sums = acc[target]
            for j in range(0, total, 2):
                left = jnp.concatenate(
                    [
                        jnp.where(group == code_s[level, jj] - target * n_chain, tiled, 0.0).astype(BF16)
                        for jj in (j, j + 1)
                    ],
                    axis=1,
                )
                right = fb[slot[level], pl.ds(j, 2)].reshape(2 * width, width)
                sums = sums + jnp.dot(left, right, preferred_element_type=F32)
            acc[target] = sums

        spread(level - 1)
        own = [
            pltpu.make_async_remote_copy(
                src_ref=acc.at[level - 1, pl.ds(lane(d) * part, part)],
                dst_ref=acc_recv.at[level - 1, d],
                send_sem=ac_send.at[level - 1, d],
                recv_sem=ac_recv.at[level - 1, d],
                device_id={"chain": lane(d)},
                device_id_type=MESH,
            )
            for d in range(1, n_chain)
        ]
        for copy in own:
            copy.start()
        if level == levels - 1:
            half_copies = share(half_tx, half_rx, half_lv, ho_send, ho_recv)
        for target in range(level - 1):
            spread(target)

    sol_copies = share(sol_tx, sol_rx, sol_lv, so_send, so_recv)

    def collect(tx, rx, copies, out, wide):
        for row in range(rows):
            wide[row, pl.ds(k * part, part)] = tx[row].astype(F32)
        for d in range(1, n_col):
            copies[d - 1].wait_recv()
            for row in range(rows):
                wide[row, pl.ds(column(n_col - d) * part, part)] = rx[d, row].astype(F32)
        for row in range(rows):
            out[row, 0] = wide[row].astype(BF16)

    collect(half_tx, half_rx, half_copies, half_out, rhs_f)
    collect(sol_tx, sol_rx, sol_copies, solved_out, rhs_f)
    for copy in pending + pat_copies + far_copies + near_copies + forwards + half_copies + sol_copies:
        copy.wait_send()


def per_device(n_chain, n_col, rhs, pattern, factor, inverse, level_size):
    rows, _, probes, width = rhs.shape
    entries = factor.shape[2]
    levels = level_size.shape[0]
    part = probes // n_col
    total = entries * n_col
    dma = pltpu.SemaphoreType.DMA
    vmem = pl.BlockSpec(memory_space=pltpu.VMEM)
    out = jax.ShapeDtypeStruct(rhs.shape, rhs.dtype)
    return pl.pallas_call(
        functools.partial(kernel, n_chain, n_col, levels),
        out_shape=(out, out),
        in_specs=[
            vmem,
            vmem,
            pl.BlockSpec(memory_space=pl.ANY),
            vmem,
            pl.BlockSpec(memory_space=pltpu.SMEM),
        ],
        out_specs=(vmem, vmem),
        scratch_shapes=[
            pltpu.VMEM((rows, total, width, width), BF16),
            pltpu.VMEM((n_col, rows, 1, entries), jnp.int32),
            pltpu.SMEM((n_col, rows, 1, entries), jnp.int32),
            pltpu.SMEM((levels, total), jnp.int32),
            pltpu.VMEM((rows, probes, width), F32),
            pltpu.VMEM((levels * n_chain, part, width), F32),
            pltpu.VMEM((levels, part, width), BF16),
            pltpu.VMEM((levels, n_chain, part, width), BF16),
            pltpu.VMEM((levels, n_chain * part, width), F32),
            pltpu.VMEM((levels, n_chain, part, width), F32),
            pltpu.VMEM((levels, part, width), F32),
            pltpu.VMEM((levels, part, width), F32),
            pltpu.VMEM((rows, part, width), BF16),
            pltpu.VMEM((rows, part, width), BF16),
            pltpu.VMEM((n_col, rows, part, width), BF16),
            pltpu.VMEM((n_col, rows, part, width), BF16),
            dma((n_col,)),
            dma((n_col,)),
            dma((n_col,)),
            dma((rows,)),
            dma((rows,)),
            dma((rows,)),
            dma((rows,)),
            dma((rows,)),
            dma((rows,)),
            dma((rows,)),
            dma((levels, n_chain)),
            dma((levels, n_chain)),
            dma((levels, n_chain)),
            dma((levels, n_chain)),
            dma((n_col,)),
            dma((n_col,)),
            dma((n_col,)),
            dma((n_col,)),
        ],
        compiler_params=pltpu.CompilerParams(collective_id=0, has_side_effects=True),
    )(rhs, pattern, factor, inverse, level_size)


def solution(mesh):
    return jax.shard_map(
        functools.partial(per_device, mesh.shape["chain"], mesh.shape["col"]),
        mesh=mesh,
        in_specs=(
            P(None, "chain", None, None),
            P(None, "chain", "col"),
            P(None, "chain", "col", None, None),
            P(None, "chain", None, None),
            P(),
        ),
        out_specs=(P(None, "chain", None, None), P(None, "chain", None, None)),
        check_vma=False,
    )
```

```python
import functools

import jax
import jax.numpy as jnp
from jax import lax
from jax.experimental import pallas as pl
from jax.experimental.pallas import tpu as pltpu
from jax.sharding import PartitionSpec as P

MESH = pl.DeviceIdType.MESH
F32 = jnp.float32
BF16 = jnp.bfloat16


def kernel(
    n_chain,
    n_col,
    levels,
    rhs_hbm,
    pat_ref,
    fac_ref,
    inv_hbm,
    size_ref,
    half_out,
    solved_out,
    fb,
    rhs_ref,
    inv_ref,
    in_sem,
    pat_v,
    pat_s,
    code_s,
    rhs_f,
    store,
    seg_send,
    seg_recv,
    acc,
    acc_recv,
    half_lv,
    sol_lv,
    half_tx,
    sol_tx,
    half_rx,
    sol_rx,
    pat_sem,
    pat_ssem,
    pat_lsem,
    loc_sem,
    fx_send,
    fx_recv,
    fo_send,
    fo_recv,
    ff_send,
    ff_recv,
    sg_send,
    sg_recv,
    ac_send,
    ac_recv,
    ho_send,
    ho_recv,
    so_send,
    so_recv,
):
    loads = [
        pltpu.make_async_copy(rhs_hbm, rhs_ref, in_sem.at[0]),
        pltpu.make_async_copy(inv_hbm, inv_ref, in_sem.at[1]),
    ]
    for copy in loads:
        copy.start()
    rows = rhs_ref.shape[0]
    probes = rhs_ref.shape[2]
    width = rhs_ref.shape[3]
    part = probes // n_col
    entries = fac_ref.shape[2]
    total = entries * n_col
    me = lax.axis_index("chain")
    k = lax.axis_index("col")
    far = lax.rem(k + n_col // 2, n_col)
    near = k + 1 - 2 * lax.rem(k, 2)
    near_far = lax.rem(near + n_col // 2, n_col)

    def lane(d):
        return lax.rem(me + d, n_chain)

    def column(d):
        return lax.rem(k + d, n_col)

    barrier = pltpu.get_barrier_semaphore()
    for d in range(1, n_chain):
        pl.semaphore_signal(barrier, inc=1, device_id={"chain": lane(d)}, device_id_type=MESH)
    for d in range(1, n_col):
        pl.semaphore_signal(barrier, inc=1, device_id={"col": column(d)}, device_id_type=MESH)
    pl.semaphore_wait(barrier, n_chain + n_col - 2)

    pat_copies = []
    for d in range(1, n_col):
        pat_copies.append(
            pltpu.make_async_remote_copy(
                src_ref=pat_ref,
                dst_ref=pat_v.at[d],
                send_sem=pat_ssem.at[d],
                recv_sem=pat_sem.at[d],
                device_id={"col": column(d)},
                device_id_type=MESH,
            )
        )
    for copy in pat_copies:
        copy.start()
    pat_local = [pltpu.make_async_copy(pat_ref, pat_s.at[0], pat_lsem.at[0])]
    pat_local[0].start()

    def held(row, who):
        return fb.at[row, pl.ds(who * entries, entries)]

    far_copies = []
    near_copies = []
    forwards = []
    locals_ = []
    for row in range(rows):
        far_copies.append(
            pltpu.make_async_remote_copy(
                src_ref=fac_ref.at[row, 0],
                dst_ref=held(row, k),
                send_sem=fx_send.at[row],
                recv_sem=fx_recv.at[row],
                device_id={"col": far},
                device_id_type=MESH,
            )
        )
        near_copies.append(
            pltpu.make_async_remote_copy(
                src_ref=fac_ref.at[row, 0],
                dst_ref=held(row, k),
                send_sem=fo_send.at[row],
                recv_sem=fo_recv.at[row],
                device_id={"col": near},
                device_id_type=MESH,
            )
        )
        forwards.append(
            pltpu.make_async_remote_copy(
                src_ref=held(row, far),
                dst_ref=held(row, far),
                send_sem=ff_send.at[row],
                recv_sem=ff_recv.at[row],
                device_id={"col": near},
                device_id_type=MESH,
            )
        )
        locals_.append(
            pltpu.make_async_copy(fac_ref.at[row, 0], held(row, k), loc_sem.at[row])
        )
    for copy in far_copies:
        copy.start()

    ends = []
    running = jnp.int32(0)
    for level in range(levels):
        running = running + size_ref[level]
        ends.append(running)

    def level_of(position):
        found = jnp.int32(0)
        for end in ends[:-1]:
            found = found + (position >= end).astype(jnp.int32)
        return found

    own_level = [level_of(row * n_chain + me) for row in range(rows)]
    slot = []
    live = []
    for level in range(levels):
        here = jnp.int32(0)
        count = jnp.int32(0)
        for row in range(rows):
            match = own_level[row] == level
            here = jnp.where(match, row, here)
            count = count + match.astype(jnp.int32)
        slot.append(here)
        live.append(count > 0)

    for copy in loads:
        copy.wait()
    for row in range(rows):
        rhs_f[row] = rhs_ref[row, 0].astype(F32)

    def finish_forward(level, sums):
        right = rhs_f[slot[level], pl.ds(k * part, part), :]
        rest = (right - sums if sums is not None else right).astype(BF16)
        segment = lax.dot_general(
            rest, inv_ref[slot[level], 0], (((1,), (1,)), ((), ())), preferred_element_type=F32
        ).astype(BF16)
        copies = []
        if level < levels - 1:
            seg_send[level] = segment
            for d in range(1, n_chain):
                copies.append(
                    pltpu.make_async_remote_copy(
                        src_ref=seg_send.at[level],
                        dst_ref=seg_recv.at[level, d],
                        send_sem=sg_send.at[level, d],
                        recv_sem=sg_recv.at[level, d],
                        device_id={"chain": lane(d)},
                        device_id_type=MESH,
                    )
                )
            for copy in copies:
                copy.start()
        wide = segment.astype(F32)
        half_lv[level] = wide
        if level < levels - 1:
            store[level * n_chain + me] = wide
        return copies

    pending = []
    copies = finish_forward(0, None)
    for copy in near_copies:
        copy.start()
    for copy in locals_:
        copy.start()
    own = copies
    store[pl.ds(n_chain, (levels - 1) * n_chain)] = jnp.zeros(
        ((levels - 1) * n_chain, part, width), F32
    )
    acc[...] = jnp.zeros_like(acc)

    for d in range(1, n_col):
        pat_copies[d - 1].wait_recv()
        copy = pltpu.make_async_copy(pat_v.at[d], pat_s.at[d], pat_lsem.at[d])
        copy.start()
        pat_local.append(copy)
    for copy in pat_local:
        copy.wait()

    for level in range(1, levels):
        def fill(place, carry, level=level):
            who = lax.div(place, entries)
            item = lax.rem(place, entries)
            d = lax.rem(k - who + n_col, n_col)
            target = pat_s[d, slot[level], 0, item]
            code_s[level, place] = level_of(target) * n_chain + lax.rem(target, n_chain)
            return carry
        for place in range(total):
            fill(jnp.int32(place), 0)

    ready = [False] * rows

    def make_ready(upto):
        todo = [row for row in range(upto + 1) if not ready[row]]
        for row in todo:
            far_copies[row].wait_recv()
            forwards[row].start()
        for row in todo:
            locals_[row].wait()
            near_copies[row].wait_recv()
            forwards[row].wait_recv()
            ready[row] = True

    def times_rows(pieces, row):
        sums = None
        for j in range(0, total, 2):
            left = jnp.concatenate([pieces[j], pieces[j + 1]], axis=1)
            right = jnp.concatenate([fb[row, j], fb[row, j + 1]], axis=1)
            term = lax.dot_general(
                left, right, (((1,), (1,)), ((), ())), preferred_element_type=F32
            )
            sums = term if sums is None else sums + term
        return sums

    for level in range(1, levels):
        make_ready(min(level, rows - 1))
        for d in range(1, n_chain):
            own[d - 1].wait_recv()
            store[(level - 1) * n_chain + lane(n_chain - d)] = seg_recv[level - 1, d].astype(F32)
        pending += own
        pieces = [store[code_s[level, j]].astype(BF16) for j in range(total)]
        if level >= rows - 1:
            sums = times_rows(pieces, slot[level])
        else:
            sums = jnp.zeros((part, width), F32)
            for row in range(level + 1):
                sums = sums + jnp.where(slot[level] == row, times_rows(pieces, row), 0.0)
        own = finish_forward(level, sums)

    def share(tx, rx, by_level, send, recv):
        for row in range(rows):
            tx[row] = by_level[own_level[row]].astype(BF16)
        copies = [
            pltpu.make_async_remote_copy(
                src_ref=tx,
                dst_ref=rx.at[d],
                send_sem=send.at[d],
                recv_sem=recv.at[d],
                device_id={"col": column(d)},
                device_id_type=MESH,
            )
            for d in range(1, n_col)
        ]
        for copy in copies:
            copy.start()
        return copies

    group = lax.broadcasted_iota(jnp.int32, (n_chain * part, width), 0) // part
    half_copies = []
    own = []
    for level in reversed(range(levels)):
        rest = half_lv[level]
        if level < levels - 1:
            rest = rest - acc[level, pl.ds(me * part, part)]
            for d in range(1, n_chain):
                own[d - 1].wait_recv()
                rest = rest - acc_recv[level, d]
            pending += own
        solved = jnp.dot(
            rest.astype(BF16), inv_ref[slot[level], 0], preferred_element_type=F32
        ).astype(BF16).astype(F32)
        sol_lv[level] = solved
        if level == 0:
            break
        solved = jnp.where(live[level], solved, 0.0)
        tiled = jnp.concatenate([solved] * n_chain, axis=0)

        def spread(target, tiled=tiled, level=level):
            sums = acc[target]
            for j in range(0, total, 2):
                left = jnp.concatenate(
                    [
                        jnp.where(group == code_s[level, jj] - target * n_chain, tiled, 0.0).astype(BF16)
                        for jj in (j, j + 1)
                    ],
                    axis=1,
                )
                right = fb[slot[level], pl.ds(j, 2)].reshape(2 * width, width)
                sums = sums + jnp.dot(left, right, preferred_element_type=F32)
            acc[target] = sums

        spread(level - 1)
        own = [
            pltpu.make_async_remote_copy(
                src_ref=acc.at[level - 1, pl.ds(lane(d) * part, part)],
                dst_ref=acc_recv.at[level - 1, d],
                send_sem=ac_send.at[level - 1, d],
                recv_sem=ac_recv.at[level - 1, d],
                device_id={"chain": lane(d)},
                device_id_type=MESH,
            )
            for d in range(1, n_chain)
        ]
        for copy in own:
            copy.start()
        if level == levels - 1:
            half_copies = share(half_tx, half_rx, half_lv, ho_send, ho_recv)
        for target in range(level - 1):
            spread(target)

    sol_copies = share(sol_tx, sol_rx, sol_lv, so_send, so_recv)

    def collect(tx, rx, copies, out, wide):
        for row in range(rows):
            wide[row, pl.ds(k * part, part)] = tx[row].astype(F32)
        for d in range(1, n_col):
            copies[d - 1].wait_recv()
            for row in range(rows):
                wide[row, pl.ds(column(n_col - d) * part, part)] = rx[d, row].astype(F32)
        for row in range(rows):
            out[row, 0] = wide[row].astype(BF16)

    collect(half_tx, half_rx, half_copies, half_out, rhs_f)
    collect(sol_tx, sol_rx, sol_copies, solved_out, rhs_f)
    for copy in pending + pat_copies + far_copies + near_copies + forwards + half_copies + sol_copies:
        copy.wait_send()


def per_device(n_chain, n_col, rhs, pattern, factor, inverse, level_size):
    rows, _, probes, width = rhs.shape
    entries = factor.shape[2]
    levels = level_size.shape[0]
    part = probes // n_col
    total = entries * n_col
    dma = pltpu.SemaphoreType.DMA
    vmem = pl.BlockSpec(memory_space=pltpu.VMEM)
    out = pltpu.VMEM(rhs.shape, rhs.dtype)
    return pl.pallas_call(
        functools.partial(kernel, n_chain, n_col, levels),
        out_shape=(out, out),
        in_specs=[
            pl.BlockSpec(memory_space=pl.ANY),
            pl.BlockSpec(memory_space=pl.ANY),
            pl.BlockSpec(memory_space=pl.ANY),
            pl.BlockSpec(memory_space=pl.ANY),
            pl.BlockSpec(memory_space=pltpu.SMEM),
        ],
        out_specs=(vmem, vmem),
        scratch_shapes=[
            pltpu.VMEM((rows, total, width, width), BF16),
            pltpu.VMEM(rhs.shape, BF16),
            pltpu.VMEM(inverse.shape, BF16),
            dma((2,)),
            pltpu.VMEM((n_col, rows, 1, entries), jnp.int32),
            pltpu.SMEM((n_col, rows, 1, entries), jnp.int32),
            pltpu.SMEM((levels, total), jnp.int32),
            pltpu.VMEM((rows, probes, width), F32),
            pltpu.VMEM((levels * n_chain, part, width), F32),
            pltpu.VMEM((levels, part, width), BF16),
            pltpu.VMEM((levels, n_chain, part, width), BF16),
            pltpu.VMEM((levels, n_chain * part, width), F32),
            pltpu.VMEM((levels, n_chain, part, width), F32),
            pltpu.VMEM((levels, part, width), F32),
            pltpu.VMEM((levels, part, width), F32),
            pltpu.VMEM((rows, part, width), BF16),
            pltpu.VMEM((rows, part, width), BF16),
            pltpu.VMEM((n_col, rows, part, width), BF16),
            pltpu.VMEM((n_col, rows, part, width), BF16),
            dma((n_col,)),
            dma((n_col,)),
            dma((n_col,)),
            dma((rows,)),
            dma((rows,)),
            dma((rows,)),
            dma((rows,)),
            dma((rows,)),
            dma((rows,)),
            dma((rows,)),
            dma((levels, n_chain)),
            dma((levels, n_chain)),
            dma((levels, n_chain)),
            dma((levels, n_chain)),
            dma((n_col,)),
            dma((n_col,)),
            dma((n_col,)),
            dma((n_col,)),
        ],
        compiler_params=pltpu.CompilerParams(collective_id=0, has_side_effects=True),
    )(rhs, pattern, factor, inverse, level_size)


def solution(mesh):
    return jax.shard_map(
        functools.partial(per_device, mesh.shape["chain"], mesh.shape["col"]),
        mesh=mesh,
        in_specs=(
            P(None, "chain", None, None),
            P(None, "chain", "col"),
            P(None, "chain", "col", None, None),
            P(None, "chain", None, None),
            P(),
        ),
        out_specs=(P(None, "chain", None, None), P(None, "chain", None, None)),
        check_vma=False,
    )
```
